512 devices in a mesh: ctx: 32 (over z, core), chan: 4 (over x), dp: 4 (over y).
Axes of the slice: x: 4, y: 4, z: 16, core: 2. Of those that a mesh axis runs over, the one named last changes fastest.
Arguments:
- projected: bfloat16 [3, 16384, 8192], P(None, ('dp', 'ctx'), 'chan'), parts along dimension 1, may hold values from -6 to 6
- short_weight: float32 [7, 3, 8192], P(None, None, 'chan'), may hold values from -2 to 2
- pos_in: float32 [33, 64], replicated, may hold values from -1 to 1
- pos_bias: float32 [64], replicated, may hold values from -4 to 4
- sine_freq: float32 [64], replicated, may hold values from 1.5 to 3
- pos_mid: float32 [64, 64], replicated, may hold values from -0.75 to 0.75
- pos_out: float32 [64, 8192], P(None, 'chan'), may hold values from -0.75 to 0.75
- decay_rate: float32 [8192], P('chan'), may hold values from 2.4414063e-05 to 0.05
- skip_gain: float32 [8192], P('chan'), may hold values from -4 to 4
Outputs:
- mixed: bfloat16 [16384, 8192], P(('dp', 'ctx'), 'chan'), parts along dimension 0
The draws below stay inside these ranges and needn't reach their ends.
There are 4 independent parts, one for each index of `dp`. The reference program is written for one: setup_inputs(seed, part) draws one part's arguments, and reference() takes and returns one part's arrays. A program takes and returns all parts, laid end to end along the dimension named above; an argument that names none is the same for every part. Nothing has to cross between parts.
All inputs are finite; a program needn't handle non-finite values.
Results may differ from the reference program's by a relative error of at most 0.001.
Values may be sent and summed in bfloat16 or wider, within the bound.
A program may use at most 128 MiB of HBM per device.

```python
import math
import jax
import jax.numpy as jnp
from jax import lax

D = 8192
ORDER = 64
BANDS = 16
TAPS = 7
FEAT = 33
LEN = 4096


def draw_decay_rate(key, part):
    level_key = jax.random.fold_in(key, 0)
    lowest = jnp.log(jnp.float32(0.1 / LEN))
    highest = jnp.log(jnp.float32(0.05))
    levels = jax.random.uniform(level_key, (D,), jnp.float32)
    return jnp.exp(lowest + levels * (highest - lowest))


def shard_levels(stream_key, dims, cuts, low, largest):
    gain = 1.0
    for axis_at, parts in cuts:
        heights = jax.random.uniform(jax.random.fold_in(jax.random.fold_in(stream_key, 6), axis_at), (parts,), jnp.float32, low / len(cuts), largest / len(cuts))
        gain = gain * jnp.repeat(jnp.exp(heights), dims[axis_at] // parts).reshape((-1,) + (1,) * (len(dims) - 1 - axis_at))
    return gain


def centred(stream_key, shape, deviation, reach, cuts=(), held_as=jnp.bfloat16):
    loudness = shard_levels(stream_key, shape, cuts, -0.22, 0.18) if cuts else 1.0
    drawn = jax.random.normal(stream_key, shape, jnp.float32) * deviation * loudness
    return jnp.minimum(jnp.maximum(drawn, -reach), reach).astype(held_as)


def setup_inputs(seed: int = 0, part: int = 0) -> dict:
    seeds = jax.random.split(jax.random.key(seed), 10)
    part_splits = jax.random.split(jax.random.fold_in(seeds[9], part), 10)
    projected = centred(part_splits[0], (3, LEN, D), 1.0, 6.0, ((1, 32), (2, 4)))
    short_weight = centred(seeds[1], (TAPS, 3, D), TAPS ** -0.5, 2.0, ((2, 4),), jnp.float32)
    pos_in = jnp.clip(jax.random.uniform(seeds[2], (FEAT, ORDER), jnp.float32, -1.0, 1.0), -1.0, 1.0)
    pos_bias = centred(seeds[3], (ORDER,), 1.0, 4.0, (), jnp.float32)
    sine_freq = jnp.clip(jax.random.uniform(seeds[4], (ORDER,), jnp.float32, 1.5, 3.0), 1.5, 3.0)
    pos_mid = jnp.clip(jax.random.uniform(seeds[5], (ORDER, ORDER), jnp.float32, -0.75, 0.75), -0.75, 0.75)
    pos_out = centred(seeds[6], (ORDER, D), ORDER ** -0.5, 0.75, ((1, 4),), jnp.float32)
    decay_rate = draw_decay_rate(jax.random.fold_in(seeds[9], 71), part)
    skip_gain = centred(seeds[8], (D,), 1.0, 4.0, ((0, 4),), jnp.float32)
    return {"projected": projected, "short_weight": short_weight, "pos_in": pos_in, "pos_bias": pos_bias, "sine_freq": sine_freq, "pos_mid": pos_mid, "pos_out": pos_out, "decay_rate": decay_rate, "skip_gain": skip_gain}


def features(positions, total_len):
    band_ids = jnp.arange(1, BANDS + 1, dtype=jnp.float32)
    angles = positions[:, None] * band_ids[None, :] * (2.0 * math.pi / total_len)
    return jnp.concatenate([positions[:, None] / total_len, jnp.cos(angles), jnp.sin(angles)], axis=1)

def filter_rows(positions, total_len, pos_in, pos_bias, sine_freq, pos_mid, pos_out, decay_rate):
    highest = lax.Precision.HIGHEST
    inputs = features(positions, total_len)
    first_layer = jnp.sin(sine_freq * (jnp.dot(inputs, pos_in, precision=highest, preferred_element_type=jnp.float32) + pos_bias))
    second_layer = jnp.sin(sine_freq * jnp.dot(first_layer, pos_mid, precision=highest, preferred_element_type=jnp.float32))
    raw_filter = jnp.dot(second_layer, pos_out, precision=highest, preferred_element_type=jnp.float32)
    return raw_filter * jnp.exp(-decay_rate[None, :] * positions[:, None])

def short_conv(projected, short_weight):
    padded = jnp.pad(projected.astype(jnp.float32), ((0, 0), (TAPS - 1, 0), (0, 0)))
    summed = jnp.zeros(projected.shape, jnp.float32)
    for tap_index in range(TAPS):
        offset = TAPS - 1 - tap_index
        summed = summed + short_weight[tap_index][:, None, :] * padded[:, offset:offset + LEN, :]
    return summed

def causal_conv(normed, driven):
    channel_count = normed.shape[1]
    block_width = math.gcd(channel_count, 512)
    block_count = channel_count // block_width

    def one_block(block_index):
        offset = block_index * block_width
        filter_part = lax.dynamic_slice_in_dim(normed, offset, block_width, 1)
        signal_part = lax.dynamic_slice_in_dim(driven, offset, block_width, 1)
        signal_spec = jnp.fft.rfft(signal_part, n=2 * LEN, axis=0)
        filter_spec = jnp.fft.rfft(filter_part, n=2 * LEN, axis=0)
        return jnp.fft.irfft(signal_spec * filter_spec, n=2 * LEN, axis=0)[:LEN].astype(jnp.float32)
    results = lax.map(one_block, jnp.arange(block_count, dtype=jnp.int32))
    return jnp.moveaxis(results, 0, 1).reshape(LEN, channel_count)

def reference(projected, short_weight, pos_in, pos_bias, sine_freq, pos_mid, pos_out, decay_rate, skip_gain):
    short_out = short_conv(projected, short_weight)
    left_gate, right_gate, value_stream = (short_out[0], short_out[1], short_out[2])
    driven = left_gate * value_stream
    positions = jnp.arange(LEN, dtype=jnp.float32)
    long_filter = filter_rows(positions, LEN, pos_in, pos_bias, sine_freq, pos_mid, pos_out, decay_rate)
    normed = long_filter / jnp.sqrt(lax.optimization_barrier(jnp.sum(long_filter * long_filter, axis=0)) + 1e-05)
    long_conv = causal_conv(normed, driven)
    return (right_gate * (long_conv + skip_gain[None, :] * driven)).astype(jnp.bfloat16)
```

```python
import math

import jax
import jax.numpy as jnp
import numpy as np
from jax import lax
from jax.experimental import pallas as pl
from jax.experimental.pallas import tpu as pltpu
from jax.sharding import PartitionSpec as P

BANDS = 16
TAPS = 7
LANES = 128
EDGE = 8
CHUNKS = 2
HIGHEST = lax.Precision.HIGHEST
MESH = pl.DeviceIdType.MESH

OUT_POWER = 12
BACK_POWER = 10
OUT_SPAN = 248.0 / OUT_POWER
BACK_SPAN = 248.0 / BACK_POWER
OUT_LOW = 2.0 ** (-OUT_SPAN / 2)
BACK_LOW = 2.0 ** (-BACK_SPAN / 2)
OUT_REACH = (2.0**OUT_SPAN - 1.0) * OUT_LOW
BACK_REACH = (2.0**BACK_SPAN - 1.0) * BACK_LOW
LARGEST = 6.0


def position_table(total_len, rows):
    positions = np.arange(total_len, dtype=np.float32)
    bands = np.arange(1, BANDS + 1, dtype=np.float32)
    angles = positions[None, :] * bands[:, None] * np.float32(2.0 * math.pi / total_len)
    angles = angles.astype(np.float32).astype(np.float64)
    table = np.zeros((rows, total_len), np.float32)
    table[0] = positions / np.float32(total_len)
    table[1 : 1 + BANDS] = np.cos(angles)
    table[1 + BANDS : 1 + 2 * BANDS] = np.sin(angles)
    table[1 + 2 * BANDS] = 1.0
    return table


def two_parts(table):
    high = table.astype(jnp.bfloat16)
    low = (table - high.astype(np.float64)).astype(jnp.bfloat16)
    return high, low


def inner_tables():
    ids = np.arange(LANES, dtype=np.float64)
    angles = 2.0 * math.pi / LANES * np.mod(ids[:, None] * ids[None, :], LANES)
    cos, sin = np.cos(angles), np.sin(angles)
    forth = np.block([[cos, -sin], [sin, cos]])
    back = np.block([[cos, sin], [-sin, cos]])
    return np.stack(two_parts(forth) + two_parts(back))


def twist_table(outer, total_len):
    angles = (
        2.0
        * math.pi
        / total_len
        * (np.arange(outer)[:, None] + 0.25)
        * np.arange(LANES)[None, :]
    )
    return np.stack([np.cos(angles), np.sin(angles)], axis=1).astype(np.float32)


def turned(real, imag, cos, sin):
    if abs(sin) < 1e-12 and cos > 0:
        return real, imag
    if abs(cos) < 1e-12:
        return (-imag, real) if sin > 0 else (imag, -real)
    if abs(abs(cos) - abs(sin)) < 1e-12 and cos > 0:
        half = math.sqrt(0.5)
        if sin > 0:
            return (real - imag) * half, (real + imag) * half
        return (real + imag) * half, (imag - real) * half
    return real * cos - imag * sin, real * sin + imag * cos


def short_fourier(items, sign):
    size = len(items)
    if size == 1:
        return items
    even = short_fourier(items[0::2], sign)
    odd = short_fourier(items[1::2], sign)
    first, second = [], []
    for at in range(size // 2):
        angle = sign * 2.0 * math.pi * at / size
        real, imag = turned(odd[at][0], odd[at][1], math.cos(angle), math.sin(angle))
        first.append((even[at][0] + real, even[at][1] + imag))
        second.append((even[at][0] - real, even[at][1] - imag))
    return first + second


def sine(x):
    turns = jnp.round(x * (1.0 / math.pi))
    r = x - turns * 3.140625
    r = r - turns * 9.67502593994140625e-4
    r = r - turns * 1.509957990978376432e-7
    s = r * r
    poly = -2.38898859e-8 * s + 2.75255613e-6
    poly = poly * s - 1.98408743e-4
    poly = poly * s + 8.33333310e-3
    poly = poly * s - 1.66666667e-1
    value = r + r * s * poly
    half = turns * 0.5
    odd = half - jnp.floor(half)
    return value * (1.0 - 4.0 * odd)


def coded(value, scale, low, power):
    w = low + jnp.abs(value) * scale
    two = w * w
    four = two * two
    eight = four * four
    if power == 12:
        top = eight * four
    else:
        top = eight * two
    return jnp.where(value < 0, -top, top)


def decoded(code, low, power):
    w = jnp.exp(jnp.log(jnp.abs(code)) * (1.0 / power)) - low
    return jnp.where(code < 0, -w, w)


def kernel(
    ctx,
    proj_any,
    weight_any,
    *refs,
):
    (
        pos_in_any,
        pos_bias_any,
        sine_freq_any,
        pos_mid_any,
        pos_out_any,
        decay_any,
        skip_any,
        feats_any,
        inner_any,
        twist_any,
        out,
        proj,
        weight,
        pos_in,
        pos_bias,
        sine_freq,
        pos_mid,
        pos_out,
        decay,
        skip,
        feats,
        inner,
        twist,
        wide,
        driven,
        rim,
        first_w,
        second_w,
        second,
        own_out,
        own_decay,
        values,
        spec,
        filt,
        send_f,
        got_f,
        send_r,
        got_r,
        local_sem,
        rim_send,
        rim_recv,
        f_send,
        f_recv,
        r_send,
        r_recv,
    ) = refs
    me = lax.axis_index("ctx")
    chip = lax.div(me, 2)
    core = lax.rem(me, 2)
    chips = ctx // 2
    rows = proj.shape[1]
    own = got_f.shape[2]
    total_len = ctx * rows

    early = ((weight_any, weight), (proj_any, proj))
    late = (
        (pos_in_any, pos_in),
        (pos_bias_any, pos_bias),
        (sine_freq_any, sine_freq),
        (pos_mid_any, pos_mid),
        (pos_out_any, pos_out),
        (decay_any, decay),
        (skip_any, skip),
        (feats_any, feats),
        (inner_any, inner),
        (twist_any, twist),
    )
    fetches = [
        pltpu.make_async_copy(there, here, local_sem.at[i])
        for i, (there, here) in enumerate(early + late)
    ]
    for fetch in fetches:
        fetch.start()

    barrier = pltpu.get_barrier_semaphore()

    def greet(i, carry):
        pl.semaphore_signal(
            barrier, inc=1, device_id={"ctx": lax.rem(me + i, ctx)}, device_id_type=MESH
        )
        return carry

    lax.fori_loop(1, ctx, greet, 0)

    def slab(n):
        return pl.ds(pl.multiple_of(n * LANES, LANES), LANES)

    def taps_sum(stream, n, start, count):
        total = None
        for tap in range(TAPS):
            part = weight[stream, pl.ds(tap, 1), slab(n)] * wide[
                stream, n, EDGE + start - tap : EDGE + start - tap + count, :
            ]
            total = part if total is None else total + part
        return total

    for fetch in fetches[: len(early)]:
        fetch.wait()

    def widen(n, carry):
        for stream in range(3):
            wide[stream, n, EDGE : EDGE + rows, :] = proj[stream, :, slab(n)].astype(jnp.float32)
        driven[n, EDGE:rows, :] = taps_sum(0, n, EDGE, rows - EDGE) * taps_sum(
            2, n, EDGE, rows - EDGE
        )
        return carry

    lax.fori_loop(0, chips, widen, 0)

    pl.semaphore_wait(barrier, ctx - 1)

    rim_copy = pltpu.make_async_remote_copy(
        src_ref=proj.at[:, pl.ds(rows - EDGE, EDGE), :],
        dst_ref=rim,
        send_sem=rim_send,
        recv_sem=rim_recv,
        device_id={"ctx": lax.rem(me + 1, ctx)},
        device_id_type=MESH,
    )

    @pl.when(me < ctx - 1)
    def _():
        rim_copy.start()

    @pl.when(me == 0)
    def _():
        rim[...] = jnp.zeros_like(rim)

    @pl.when(me > 0)
    def _():
        rim_copy.wait_recv()

    def forth(g, to):
        return pltpu.make_async_remote_copy(
            src_ref=send_f.at[g, to],
            dst_ref=got_f.at[g, me],
            send_sem=f_send.at[g],
            recv_sem=f_recv.at[g, me],
            device_id={"ctx": to},
            device_id_type=MESH,
        )

    def back(g, to):
        return pltpu.make_async_remote_copy(
            src_ref=send_r.at[g, to],
            dst_ref=got_r.at[g, me],
            send_sem=r_send.at[g],
            recv_sem=r_recv.at[g, me],
            device_id={"ctx": to},
            device_id_type=MESH,
        )

    def to_chip(i):
        far = chips // 2 - lax.div(i + 1, 2)
        away = jnp.where(lax.rem(i, 2) == 1, far, chips - far)
        return lax.rem(chip + away, chips)

    def bound(n):
        total = 1.0
        for stream in (0, 2):
            size = None
            for tap in range(TAPS):
                part = jnp.abs(weight[stream, pl.ds(tap, 1), slab(n)])
                size = part if size is None else size + part
            total = total * (size * LARGEST)
        return jnp.maximum(total, 1e-30)

    def push(make, g, n):
        for c in range(2):
            to = 2 * n + c

            @pl.when(to != me)
            def _():
                make(g, to).start()

    def encode(i, carry):
        n = to_chip(i)
        for stream in range(3):
            wide[stream, n, 0:EDGE, :] = rim[stream, :, slab(n)].astype(jnp.float32)
        driven[n, 0:EDGE, :] = taps_sum(0, n, 0, EDGE) * taps_sum(2, n, 0, EDGE)
        code = coded(driven[n], OUT_REACH / bound(n), OUT_LOW, OUT_POWER)
        code = code.T.astype(jnp.bfloat16)
        for c in range(2):
            for g in range(CHUNKS):
                low = (c * CHUNKS + g) * own
                send_f[g, 2 * n + c] = code[low : low + own]
        push(forth, 0, n)
        return carry

    lax.fori_loop(0, chips, encode, 0)

    def rest(g, make):
        def step(i, carry):
            push(make, g, to_chip(i))
            return carry

        lax.fori_loop(0, chips, step, 0)

    for g in range(1, CHUNKS):
        rest(g, forth)
    for g in range(CHUNKS):
        got_f[g, me] = send_f[g, me]

    for fetch in fetches[len(early) :]:
        fetch.wait()
    taps_in = pos_in.shape[0]
    freq = sine_freq[...]
    first_w[...] = jnp.zeros_like(first_w)
    first_w[0:taps_in, :] = pos_in[...] * freq
    first_w[taps_in : taps_in + 1, :] = pos_bias[...] * freq
    second_w[...] = pos_mid[...] * freq
    turn = (((0,), (0,)), ((), ()))
    span = 512

    def network(j, carry):
        at = pl.ds(pl.multiple_of(j * span, span), span)
        one = sine(
            lax.dot_general(
                first_w[...],
                feats[:, at],
                turn,
                precision=HIGHEST,
                preferred_element_type=jnp.float32,
            )
        )
        second[:, at] = sine(
            lax.dot_general(
                second_w[...], one, turn, precision=HIGHEST, preferred_element_type=jnp.float32
            )
        )
        return carry

    lax.fori_loop(0, total_len // span, network, 0)
    own_out[...] = pos_out[:, slab(chip)].T
    own_decay[...] = jnp.broadcast_to(decay[:, slab(chip)], (LANES, LANES)).T

    group = 8

    def halves(x):
        high = x.astype(jnp.bfloat16)
        return high, (x - high.astype(jnp.float32)).astype(jnp.bfloat16)

    def product(x, which):
        high, low = halves(x)
        return (
            jnp.dot(high, inner[which], preferred_element_type=jnp.float32)
            + jnp.dot(low, inner[which], preferred_element_type=jnp.float32)
            + jnp.dot(high, inner[which + 1], preferred_element_type=jnp.float32)
        )

    def outer_forth():
        def step(j, carry):
            at = pl.ds(pl.multiple_of(j * group, group), group)
            items = []
            for a in range(ctx):
                x = values[a, at, :]
                angle = 2.0 * math.pi * a / (4 * ctx)
                items.append((x * math.cos(angle), x * -math.sin(angle)))
            for k, (real, imag) in enumerate(short_fourier(items, -1)):
                cos, sin = twist[k, 0:1, :], twist[k, 1:2, :]
                spec[k, at, 0:LANES] = real * cos + imag * sin
                spec[k, at, LANES : 2 * LANES] = imag * cos - real * sin
            return carry

        lax.fori_loop(0, own // group, step, 0)

    def outer_back():
        def step(j, carry):
            at = pl.ds(pl.multiple_of(j * group, group), group)
            items = []
            for k in range(ctx):
                real, imag = spec[k, at, 0:LANES], spec[k, at, LANES : 2 * LANES]
                cos, sin = twist[k, 0:1, :], twist[k, 1:2, :]
                items.append((real * cos - imag * sin, imag * cos + real * sin))
            for a, (real, imag) in enumerate(short_fourier(items, 1)):
                angle = 2.0 * math.pi * a / (4 * ctx)
                values[a, at, :] = real * math.cos(angle) - imag * math.sin(angle)
            return carry

        lax.fori_loop(0, own // group, step, 0)

    for g in range(CHUNKS):
        low = pl.ds(pl.multiple_of(core * (CHUNKS * own) + g * own, own), own)
        out_rows = own_out[low, :]
        out_high, out_low = halves(out_rows)
        rate = own_decay[low, :]

        def fill(a, squares):
            at = slab(a)
            high, less = halves(second[:, at])
            raw = (
                jnp.dot(out_high, high, preferred_element_type=jnp.float32)
                + jnp.dot(out_low, high, preferred_element_type=jnp.float32)
                + jnp.dot(out_high, less, preferred_element_type=jnp.float32)
            )
            place = lax.broadcasted_iota(jnp.int32, (own, LANES), 1) + a * LANES
            long_filter = raw * jnp.exp(-(rate * place.astype(jnp.float32)))
            values[a] = long_filter
            return squares + long_filter * long_filter

        squares = lax.fori_loop(0, ctx, fill, jnp.zeros((own, LANES), jnp.float32))
        norm = jnp.sqrt(jnp.sum(squares, axis=1, keepdims=True) + 1e-05)
        scale = (1.0 / total_len) / norm
        outer_forth()
        full = product(spec[...].reshape(ctx * own, 2 * LANES), 0)
        filt[g] = full.reshape(ctx, own, 2 * LANES) * scale[None]

    for g in range(CHUNKS):

        def arrive(i, carry):
            frm = lax.rem(me + i, ctx)
            pltpu.make_async_remote_copy(
                src_ref=send_f.at[g, frm],
                dst_ref=got_f.at[g, frm],
                send_sem=f_send.at[g],
                recv_sem=f_recv.at[g, frm],
                device_id={"ctx": frm},
                device_id_type=MESH,
            ).wait_recv()
            return carry

        lax.fori_loop(1, ctx, arrive, 0)

        def decode(a, carry):
            values[a] = decoded(got_f[g, a].astype(jnp.float32), OUT_LOW, OUT_POWER)
            return carry

        lax.fori_loop(0, ctx, decode, 0)
        outer_forth()
        full = product(spec[...].reshape(ctx * own, 2 * LANES), 0)
        real, imag = full[:, :LANES], full[:, LANES:]
        response = filt[g].reshape(ctx * own, 2 * LANES)
        f_real, f_imag = response[:, :LANES], response[:, LANES:]
        mixed_real = real * f_real - imag * f_imag
        mixed_imag = real * f_imag + imag * f_real
        full = product(jnp.concatenate([mixed_real, mixed_imag], axis=1), 2)
        spec[...] = full.reshape(ctx, own, 2 * LANES)
        outer_back()

        def pack(i, carry):
            n = to_chip(i)
            for c in range(2):
                a = 2 * n + c
                code = coded(values[a], BACK_REACH / (64.0 * OUT_REACH), BACK_LOW, BACK_POWER)
                send_r[g, a] = code.astype(jnp.bfloat16)
            push(back, g, n)
            return carry

        lax.fori_loop(0, chips, pack, 0)
        got_r[g, me] = send_r[g, me]

    def gate(n, carry):
        wide[1, n, EDGE : EDGE + rows, :] = taps_sum(1, n, 0, rows)
        return carry

    lax.fori_loop(0, chips, gate, 0)

    def finish(i, carry):
        n = to_chip(chips - 1 - i)
        parts = []
        for c in range(2):
            frm = 2 * n + c
            for g in range(CHUNKS):

                @pl.when(frm != me)
                def _():
                    pltpu.make_async_remote_copy(
                        src_ref=send_r.at[g, frm],
                        dst_ref=got_r.at[g, frm],
                        send_sem=r_send.at[g],
                        recv_sem=r_recv.at[g, frm],
                        device_id={"ctx": frm},
                        device_id_type=MESH,
                    ).wait_recv()

        for c in range(2):
            for g in range(CHUNKS):
                parts.append(got_r[g, 2 * n + c].astype(jnp.float32))
        code = jnp.concatenate(parts, axis=0).T
        unit = bound(n) * (64.0 / BACK_REACH)
        long_conv = decoded(code, BACK_LOW, BACK_POWER) * unit
        right = wide[1, n, EDGE : EDGE + rows, :]
        mixed = right * (long_conv + skip[:, slab(n)] * driven[n])
        out[:, slab(n)] = mixed.astype(jnp.bfloat16)
        return carry

    lax.fori_loop(0, chips, finish, 0)

    @pl.when(me < ctx - 1)
    def _():
        rim_copy.wait_send()

    for g in range(CHUNKS):
        for buffer, sem in ((send_f, f_send), (send_r, r_send)):
            sent = buffer.at[g, pl.ds(0, ctx - 1)]
            pltpu.make_async_remote_copy(
                src_ref=sent,
                dst_ref=sent,
                send_sem=sem.at[g],
                recv_sem=sem.at[g],
                device_id={"ctx": me},
                device_id_type=MESH,
            ).wait_send()


def body(
    projected, short_weight, pos_in, pos_bias, sine_freq, pos_mid, pos_out, decay_rate, skip_gain
):
    ctx = lax.axis_size("ctx")
    _, rows, width = projected.shape
    own = width // ctx // CHUNKS
    order = pos_mid.shape[0]
    total_len = ctx * rows
    feat_rows = -(-(pos_in.shape[0] + 1) // 8) * 8
    feats = jnp.asarray(position_table(total_len, feat_rows))
    inner = jnp.asarray(inner_tables())
    twist = jnp.asarray(twist_table(ctx, total_len))
    vmem = pl.BlockSpec(memory_space=pltpu.VMEM)
    left = pl.BlockSpec(memory_space=pltpu.HBM)
    bf16, f32 = jnp.bfloat16, jnp.float32
    dma = pltpu.SemaphoreType.DMA
    wires = [pltpu.VMEM((CHUNKS, ctx, own, rows), bf16)] * 4

    def call(*refs):
        return kernel(ctx, *refs)

    operands = (
        projected,
        short_weight.transpose(1, 0, 2),
        pos_in,
        pos_bias.reshape(1, -1),
        sine_freq.reshape(1, -1),
        pos_mid,
        pos_out,
        decay_rate.reshape(1, -1),
        skip_gain.reshape(1, -1),
        feats,
        inner,
        twist,
    )
    return pl.pallas_call(
        call,
        out_shape=jax.ShapeDtypeStruct((rows, width), bf16),
        in_specs=[left] * 12,
        out_specs=vmem,
        scratch_shapes=[
            *[pltpu.VMEM(operand.shape, operand.dtype) for operand in operands],
            pltpu.VMEM((3, width // LANES, EDGE + rows, LANES), f32),
            pltpu.VMEM((width // LANES, rows, LANES), f32),
            pltpu.VMEM((3, EDGE, width), bf16),
            pltpu.VMEM((feat_rows, order), f32),
            pltpu.VMEM((order, order), f32),
            pltpu.VMEM((order, total_len), f32),
            pltpu.VMEM((LANES, order), f32),
            pltpu.VMEM((LANES, LANES), f32),
            pltpu.VMEM((ctx, own, LANES), f32),
            pltpu.VMEM((ctx, own, 2 * LANES), f32),
            pltpu.VMEM((CHUNKS, ctx, own, 2 * LANES), f32),
            *wires,
            dma((len(operands),)),
            dma,
            dma,
            dma((CHUNKS,)),
            dma((CHUNKS, ctx)),
            dma((CHUNKS,)),
            dma((CHUNKS, ctx)),
        ],
        compiler_params=pltpu.CompilerParams(
            collective_id=0, has_side_effects=True, vmem_limit_bytes=60 * 1024 * 1024
        ),
        name="hyena",
    )(*operands)


def solution(mesh):
    placed = (
        P(None, ("dp", "ctx"), "chan"),
        P(None, None, "chan"),
        P(),
        P(),
        P(),
        P(),
        P(None, "chan"),
        P("chan"),
        P("chan"),
    )
    return jax.shard_map(
        body, mesh=mesh, in_specs=placed, out_specs=P(("dp", "ctx"), "chan"), check_vma=False
    )
```

```python
import math

import jax
import jax.numpy as jnp
import numpy as np
from jax import lax
from jax.experimental import pallas as pl
from jax.experimental.pallas import tpu as pltpu
from jax.sharding import PartitionSpec as P

BANDS = 16
TAPS = 7
LANES = 128
EDGE = 8
CHUNKS = 2
MESH = pl.DeviceIdType.MESH

OUT_POWER = 12
BACK_POWER = 10
OUT_SPAN = 248.0 / OUT_POWER
BACK_SPAN = 248.0 / BACK_POWER
OUT_LOW = 2.0 ** (-OUT_SPAN / 2)
BACK_LOW = 2.0 ** (-BACK_SPAN / 2)
OUT_REACH = (2.0**OUT_SPAN - 1.0) * OUT_LOW
BACK_REACH = (2.0**BACK_SPAN - 1.0) * BACK_LOW
LARGEST = 6.0


def position_table(total_len, rows):
    positions = np.arange(total_len, dtype=np.float32)
    bands = np.arange(1, BANDS + 1, dtype=np.float32)
    angles = positions[None, :] * bands[:, None] * np.float32(2.0 * math.pi / total_len)
    angles = angles.astype(np.float32).astype(np.float64)
    table = np.zeros((rows, total_len), np.float32)
    table[0] = positions / np.float32(total_len)
    table[1 : 1 + BANDS] = np.cos(angles)
    table[1 + BANDS : 1 + 2 * BANDS] = np.sin(angles)
    table[1 + 2 * BANDS] = 1.0
    return table


def two_parts(table):
    high = table.astype(jnp.bfloat16)
    low = (table - high.astype(np.float64)).astype(jnp.bfloat16)
    return high, low


LEFT_PARTS = (0, 0, 1, 0, 1, 2)
RIGHT_PARTS = (0, 1, 0, 2, 1, 0)


def stacked_positions(total_len, rows, depth):
    table = position_table(total_len, rows).astype(np.float64)
    parts = []
    for _ in range(3):
        part = table.astype(jnp.bfloat16)
        parts.append(part)
        table = table - part.astype(np.float64)
    stack = np.concatenate([parts[at] for at in RIGHT_PARTS])
    empty = np.zeros((depth - stack.shape[0], total_len), jnp.bfloat16)
    return np.concatenate([stack, empty])


def inner_tables():
    ids = np.arange(LANES, dtype=np.float64)
    angles = 2.0 * math.pi / LANES * np.mod(ids[:, None] * ids[None, :], LANES)
    cos, sin = np.cos(angles), np.sin(angles)
    forth = np.block([[cos, -sin], [sin, cos]])
    back = np.block([[cos, sin], [-sin, cos]])
    return np.stack(two_parts(forth) + two_parts(back))


def twist_table(outer, total_len):
    angles = (
        2.0
        * math.pi
        / total_len
        * (np.arange(outer)[:, None] + 0.25)
        * np.arange(LANES)[None, :]
    )
    return np.stack([np.cos(angles), np.sin(angles)], axis=1).astype(np.float32)


def turned(real, imag, cos, sin):
    if abs(sin) < 1e-12 and cos > 0:
        return real, imag
    if abs(cos) < 1e-12:
        return (-imag, real) if sin > 0 else (imag, -real)
    if abs(abs(cos) - abs(sin)) < 1e-12 and cos > 0:
        half = math.sqrt(0.5)
        if sin > 0:
            return (real - imag) * half, (real + imag) * half
        return (real + imag) * half, (imag - real) * half
    return real * cos - imag * sin, real * sin + imag * cos


def short_fourier(items, sign):
    size = len(items)
    if size == 1:
        return items
    even = short_fourier(items[0::2], sign)
    odd = short_fourier(items[1::2], sign)
    first, second = [], []
    for at in range(size // 2):
        angle = sign * 2.0 * math.pi * at / size
        real, imag = turned(odd[at][0], odd[at][1], math.cos(angle), math.sin(angle))
        first.append((even[at][0] + real, even[at][1] + imag))
        second.append((even[at][0] - real, even[at][1] - imag))
    return first + second


def sine(x):
    turns = jnp.round(x * (1.0 / math.pi))
    r = x - turns * 3.140625
    r = r - turns * 9.67502593994140625e-4
    r = r - turns * 1.509957990978376432e-7
    s = r * r
    poly = -2.38898859e-8 * s + 2.75255613e-6
    poly = poly * s - 1.98408743e-4
    poly = poly * s + 8.33333310e-3
    poly = poly * s - 1.66666667e-1
    value = r + r * s * poly
    half = turns * 0.5
    odd = half - jnp.floor(half)
    return value * (1.0 - 4.0 * odd)


def coded(value, scale, low, power):
    w = low + jnp.abs(value) * scale
    two = w * w
    four = two * two
    eight = four * four
    if power == 12:
        top = eight * four
    else:
        top = eight * two
    return jnp.where(value < 0, -top, top)


def decoded(code, low, power):
    w = jnp.exp(jnp.log(jnp.abs(code)) * (1.0 / power)) - low
    return jnp.where(code < 0, -w, w)


def kernel(
    ctx,
    feat_rows,
    proj_any,
    weight_any,
    *refs,
):
    (
        pos_in_any,
        pos_bias_any,
        sine_freq_any,
        pos_mid_any,
        pos_out_any,
        decay_any,
        skip_any,
        feats_any,
        inner_any,
        twist_any,
        out,
        proj,
        weight,
        pos_in,
        pos_bias,
        sine_freq,
        pos_mid,
        pos_out,
        decay,
        skip,
        feats,
        inner,
        twist,
        wide,
        driven,
        rim,
        first_w,
        second_w,
        third_w,
        first_t,
        second_t,
        third_t,
        own_decay,
        values,
        taps,
        spec,
        filt,
        send_f,
        got_f,
        send_r,
        got_r,
        local_sem,
        rim_send,
        rim_recv,
        f_send,
        f_recv,
        r_send,
        r_recv,
        news,
    ) = refs
    me = lax.axis_index("ctx")
    chip = lax.div(me, 2)
    core = lax.rem(me, 2)
    chips = ctx // 2
    rows = proj.shape[1]
    own = got_f.shape[2]
    total_len = ctx * rows

    early = ((weight_any, weight), (proj_any, proj))
    late = (
        (pos_in_any, pos_in),
        (pos_bias_any, pos_bias),
        (sine_freq_any, sine_freq),
        (pos_mid_any, pos_mid),
        (pos_out_any, pos_out),
        (decay_any, decay),
        (skip_any, skip),
        (feats_any, feats),
        (inner_any, inner),
        (twist_any, twist),
    )
    fetches = [
        pltpu.make_async_copy(there, here, local_sem.at[i])
        for i, (there, here) in enumerate(early + late)
    ]
    for fetch in fetches[: len(early)]:
        fetch.start()

    barrier = pltpu.get_barrier_semaphore()

    right = lax.rem(chip + 1, chips)
    left = lax.rem(chip + chips - 1, chips)

    def tell(sem, to):
        pl.semaphore_signal(sem, inc=1, device_id={"ctx": to}, device_id_type=MESH)

    near = (2 * chip + 1 - core, 2 * left, 2 * left + 1, 2 * right, 2 * right + 1)
    for to in near:
        tell(barrier, to)

    def slab(n):
        return pl.ds(pl.multiple_of(n * LANES, LANES), LANES)

    def taps_sum(stream, n, start, count):
        total = None
        for tap in range(TAPS):
            part = weight[stream, pl.ds(tap, 1), slab(n)] * wide[
                stream, n, EDGE + start - tap : EDGE + start - tap + count, :
            ]
            total = part if total is None else total + part
        return total

    pl.semaphore_wait(barrier, len(near))

    rim_copy = pltpu.make_async_remote_copy(
        src_ref=proj_any.at[:, pl.ds(rows - EDGE, EDGE), :],
        dst_ref=rim,
        send_sem=rim_send,
        recv_sem=rim_recv,
        device_id={"ctx": lax.rem(me + 1, ctx)},
        device_id_type=MESH,
    )

    def spread(step):
        away = 2**step
        tell(news.at[step, 0], 2 * lax.rem(chip + away, chips) + core)
        tell(news.at[step, 1], 2 * lax.rem(chip + chips - away, chips) + core)

    def hear(step):
        for side in range(2):
            pl.semaphore_wait(news.at[step, side], 1)

    spread(0)

    @pl.when(me < ctx - 1)
    def _():
        rim_copy.start()

    for fetch in fetches[: len(early)]:
        fetch.wait()
    for fetch in fetches[len(early) :]:
        fetch.start()

    def widen(n, carry):
        for stream in range(3):
            wide[stream, n, EDGE : EDGE + rows, :] = proj[stream, :, slab(n)].astype(jnp.float32)
        driven[n, EDGE:rows, :] = taps_sum(0, n, EDGE, rows - EDGE) * taps_sum(
            2, n, EDGE, rows - EDGE
        )
        return carry

    lax.fori_loop(0, chips // 2, widen, 0)
    hear(0)
    spread(1)
    lax.fori_loop(chips // 2, chips, widen, 0)
    hear(1)
    spread(2)

    @pl.when(me == 0)
    def _():
        rim[...] = jnp.zeros_like(rim)

    @pl.when(me > 0)
    def _():
        rim_copy.wait_recv()

    def forth(g, to):
        return pltpu.make_async_remote_copy(
            src_ref=send_f.at[g, to],
            dst_ref=got_f.at[g, me],
            send_sem=f_send.at[g],
            recv_sem=f_recv.at[g, me],
            device_id={"ctx": to},
            device_id_type=MESH,
        )

    def back(g, to):
        return pltpu.make_async_remote_copy(
            src_ref=send_r.at[g, to],
            dst_ref=got_r.at[g, me],
            send_sem=r_send.at[g],
            recv_sem=r_recv.at[g, me],
            device_id={"ctx": to},
            device_id_type=MESH,
        )

    def to_chip(i):
        far = chips // 2 - lax.div(i + 1, 2)
        away = jnp.where(lax.rem(i, 2) == 1, far, chips - far)
        return lax.rem(chip + away, chips)

    def bound(n):
        total = 1.0
        for stream in (0, 2):
            size = None
            for tap in range(TAPS):
                part = jnp.abs(weight[stream, pl.ds(tap, 1), slab(n)])
                size = part if size is None else size + part
            total = total * (size * LARGEST)
        return jnp.maximum(total, 1e-30)

    def push(make, g, n):
        for c in range(2):
            to = 2 * n + c

            @pl.when(to != me)
            def _():
                make(g, to).start()

    def encode(n):
        for stream in range(3):
            wide[stream, n, 0:EDGE, :] = rim[stream, :, slab(n)].astype(jnp.float32)
        driven[n, 0:EDGE, :] = taps_sum(0, n, 0, EDGE) * taps_sum(2, n, 0, EDGE)
        code = coded(driven[n], OUT_REACH / bound(n), OUT_LOW, OUT_POWER)
        code = code.T.astype(jnp.bfloat16)
        for c in range(2):
            for g in range(CHUNKS):
                low = (c * CHUNKS + g) * own
                send_f[g, 2 * n + c] = code[low : low + own]
        push(forth, 0, n)

    def around(first):
        def step(i, carry):
            away = first - lax.div(i, 2)
            away = jnp.where(lax.rem(i, 2) == 0, away, chips - away)
            encode(lax.rem(chip + away, chips))
            return carry

        return step

    quarter = chips // 4
    lax.fori_loop(0, 2 * quarter, around(quarter), 0)
    encode(chip)
    hear(2)
    encode(lax.rem(chip + 2 * quarter, chips))
    lax.fori_loop(0, 2 * quarter - 2, around(2 * quarter - 1), 0)

    def rest(g, make):
        def step(i, carry):
            push(make, g, to_chip(i))
            return carry

        lax.fori_loop(0, chips, step, 0)

    for g in range(1, CHUNKS):
        rest(g, forth)
    for g in range(CHUNKS):
        got_f[g, me] = send_f[g, me]

    for fetch in fetches[len(early) :]:
        fetch.wait()
    taps_in = pos_in.shape[0]
    order = pos_mid.shape[0]
    freq = sine_freq[...]

    def halves(x):
        high = x.astype(jnp.bfloat16)
        return high, (x - high.astype(jnp.float32)).astype(jnp.bfloat16)

    def thirds(x):
        high, low = halves(x)
        rest_of = x - high.astype(jnp.float32)
        return high, low, (rest_of - low.astype(jnp.float32)).astype(jnp.bfloat16)

    first_w[...] = jnp.zeros_like(first_w)
    second_w[...] = jnp.zeros_like(second_w)
    third_w[...] = jnp.zeros_like(third_w)
    entry = thirds(pos_in[...] * freq)
    offset = thirds(pos_bias[...] * freq)
    middle = thirds(pos_mid[...] * freq)
    exit_high, exit_low = halves(pos_out[:, slab(chip)])
    for i, part in enumerate(LEFT_PARTS):
        at = i * feat_rows
        first_w[at : at + taps_in, 0:order] = entry[part].astype(jnp.float32)
        first_w[at + taps_in : at + taps_in + 1, 0:order] = offset[part].astype(jnp.float32)
        second_w[i * order : (i + 1) * order, 0:order] = middle[part].astype(jnp.float32)
    for i, part in enumerate((exit_high, exit_low, exit_high)):
        third_w[i * order : (i + 1) * order, :] = part.astype(jnp.float32)
    first_t[...] = first_w[...].T[0:order].astype(jnp.bfloat16)
    second_t[...] = second_w[...].T[0:order].astype(jnp.bfloat16)
    third_t[...] = third_w[...].T
    own_decay[...] = jnp.broadcast_to(decay[:, slab(chip)], (LANES, LANES)).T

    mine = pl.ds(pl.multiple_of(core * (CHUNKS * own), CHUNKS * own), CHUNKS * own)
    third = third_t[mine, :].astype(jnp.bfloat16)
    rate = own_decay[mine, :]
    span = 512

    def network(j, squares):
        at = pl.ds(pl.multiple_of(j * span, span), span)
        one = thirds(sine(jnp.dot(first_t[...], feats[:, at], preferred_element_type=jnp.float32)))
        one = jnp.concatenate([one[part] for part in RIGHT_PARTS], axis=0)
        two = sine(jnp.dot(second_t[...], one, preferred_element_type=jnp.float32))
        high, low = halves(two)
        two = jnp.concatenate([high, high, low], axis=0)
        raw = jnp.dot(third, two, preferred_element_type=jnp.float32)
        for i in range(span // LANES):
            a = j * (span // LANES) + i
            place = lax.broadcasted_iota(jnp.int32, (CHUNKS * own, LANES), 1) + a * LANES
            long_filter = raw[:, i * LANES : (i + 1) * LANES] * jnp.exp(
                -(rate * place.astype(jnp.float32))
            )
            for g in range(CHUNKS):
                taps[g, a] = long_filter[g * own : (g + 1) * own]
            squares = squares + long_filter * long_filter
        return squares

    squares = lax.fori_loop(
        0, total_len // span, network, jnp.zeros((CHUNKS * own, LANES), jnp.float32)
    )
    norm = jnp.sqrt(jnp.sum(squares, axis=1, keepdims=True) + 1e-05)
    scale = (1.0 / total_len) / norm

    group = 8

    def product(x, which):
        high, low = halves(x)
        return (
            jnp.dot(high, inner[which], preferred_element_type=jnp.float32)
            + jnp.dot(low, inner[which], preferred_element_type=jnp.float32)
            + jnp.dot(high, inner[which + 1], preferred_element_type=jnp.float32)
        )

    def outer_forth(source):
        def step(j, carry):
            at = pl.ds(pl.multiple_of(j * group, group), group)
            items = []
            for a in range(ctx):
                x = source[a, at, :]
                angle = 2.0 * math.pi * a / (4 * ctx)
                items.append((x * math.cos(angle), x * -math.sin(angle)))
            for k, (real, imag) in enumerate(short_fourier(items, -1)):
                cos, sin = twist[k, 0:1, :], twist[k, 1:2, :]
                spec[k, at, 0:LANES] = real * cos + imag * sin
                spec[k, at, LANES : 2 * LANES] = imag * cos - real * sin
            return carry

        lax.fori_loop(0, own // group, step, 0)

    def outer_back():
        def step(j, carry):
            at = pl.ds(pl.multiple_of(j * group, group), group)
            items = []
            for k in range(ctx):
                real, imag = spec[k, at, 0:LANES], spec[k, at, LANES : 2 * LANES]
                cos, sin = twist[k, 0:1, :], twist[k, 1:2, :]
                items.append((real * cos - imag * sin, imag * cos + real * sin))
            for a, (real, imag) in enumerate(short_fourier(items, 1)):
                angle = 2.0 * math.pi * a / (4 * ctx)
                values[a, at, :] = real * math.cos(angle) - imag * math.sin(angle)
            return carry

        lax.fori_loop(0, own // group, step, 0)

    for g in range(CHUNKS):
        outer_forth(taps.at[g])
        full = product(spec[...].reshape(ctx * own, 2 * LANES), 0)
        filt[g] = full.reshape(ctx, own, 2 * LANES) * scale[None, g * own : (g + 1) * own]

    for g in range(CHUNKS):

        def arrive(i, carry):
            frm = lax.rem(me + i, ctx)
            pltpu.make_async_remote_copy(
                src_ref=send_f.at[g, frm],
                dst_ref=got_f.at[g, frm],
                send_sem=f_send.at[g],
                recv_sem=f_recv.at[g, frm],
                device_id={"ctx": frm},
                device_id_type=MESH,
            ).wait_recv()
            return carry

        lax.fori_loop(1, ctx, arrive, 0)

        def decode(a, carry):
            values[a] = decoded(got_f[g, a].astype(jnp.float32), OUT_LOW, OUT_POWER)
            return carry

        lax.fori_loop(0, ctx, decode, 0)
        outer_forth(values)
        full = product(spec[...].reshape(ctx * own, 2 * LANES), 0)
        real, imag = full[:, :LANES], full[:, LANES:]
        response = filt[g].reshape(ctx * own, 2 * LANES)
        f_real, f_imag = response[:, :LANES], response[:, LANES:]
        mixed_real = real * f_real - imag * f_imag
        mixed_imag = real * f_imag + imag * f_real
        full = product(jnp.concatenate([mixed_real, mixed_imag], axis=1), 2)
        spec[...] = full.reshape(ctx, own, 2 * LANES)
        outer_back()

        def pack(i, carry):
            n = to_chip(i)
            for c in range(2):
                a = 2 * n + c
                code = coded(values[a], BACK_REACH / (64.0 * OUT_REACH), BACK_LOW, BACK_POWER)
                send_r[g, a] = code.astype(jnp.bfloat16)
            push(back, g, n)
            return carry

        lax.fori_loop(0, chips, pack, 0)
        got_r[g, me] = send_r[g, me]

    def gate(n, carry):
        wide[1, n, EDGE : EDGE + rows, :] = taps_sum(1, n, 0, rows)
        return carry

    lax.fori_loop(0, chips, gate, 0)

    def finish(i, carry):
        n = to_chip(chips - 1 - i)
        parts = []
        for c in range(2):
            frm = 2 * n + c
            for g in range(CHUNKS):

                @pl.when(frm != me)
                def _():
                    pltpu.make_async_remote_copy(
                        src_ref=send_r.at[g, frm],
                        dst_ref=got_r.at[g, frm],
                        send_sem=r_send.at[g],
                        recv_sem=r_recv.at[g, frm],
                        device_id={"ctx": frm},
                        device_id_type=MESH,
                    ).wait_recv()

        for c in range(2):
            for g in range(CHUNKS):
                parts.append(got_r[g, 2 * n + c].astype(jnp.float32))
        code = jnp.concatenate(parts, axis=0).T
        unit = bound(n) * (64.0 / BACK_REACH)
        long_conv = decoded(code, BACK_LOW, BACK_POWER) * unit
        right = wide[1, n, EDGE : EDGE + rows, :]
        mixed = right * (long_conv + skip[:, slab(n)] * driven[n])
        out[:, slab(n)] = mixed.astype(jnp.bfloat16)
        return carry

    lax.fori_loop(0, chips, finish, 0)

    @pl.when(me < ctx - 1)
    def _():
        rim_copy.wait_send()

    for g in range(CHUNKS):
        for buffer, sem in ((send_f, f_send), (send_r, r_send)):
            sent = buffer.at[g, pl.ds(0, ctx - 1)]
            pltpu.make_async_remote_copy(
                src_ref=sent,
                dst_ref=sent,
                send_sem=sem.at[g],
                recv_sem=sem.at[g],
                device_id={"ctx": me},
                device_id_type=MESH,
            ).wait_send()


def body(
    projected, short_weight, pos_in, pos_bias, sine_freq, pos_mid, pos_out, decay_rate, skip_gain
):
    ctx = lax.axis_size("ctx")
    _, rows, width = projected.shape
    own = width // ctx // CHUNKS
    order = pos_mid.shape[0]
    total_len = ctx * rows
    feat_rows = -(-(pos_in.shape[0] + 1) // 8) * 8
    depth = -(-feat_rows * len(LEFT_PARTS) // 256) * 256
    feats = jnp.asarray(stacked_positions(total_len, feat_rows, depth))
    inner = jnp.asarray(inner_tables())
    twist = jnp.asarray(twist_table(ctx, total_len))
    vmem = pl.BlockSpec(memory_space=pltpu.VMEM)
    left = pl.BlockSpec(memory_space=pltpu.HBM)
    bf16, f32 = jnp.bfloat16, jnp.float32
    dma = pltpu.SemaphoreType.DMA
    wires = [pltpu.VMEM((CHUNKS, ctx, own, rows), bf16)] * 4

    def call(*refs):
        return kernel(ctx, feat_rows, *refs)

    operands = (
        projected,
        short_weight.transpose(1, 0, 2),
        pos_in,
        pos_bias.reshape(1, -1),
        sine_freq.reshape(1, -1),
        pos_mid,
        pos_out,
        decay_rate.reshape(1, -1),
        skip_gain.reshape(1, -1),
        feats,
        inner,
        twist,
    )
    return pl.pallas_call(
        call,
        out_shape=jax.ShapeDtypeStruct((rows, width), bf16),
        in_specs=[left] * 12,
        out_specs=vmem,
        scratch_shapes=[
            *[pltpu.VMEM(operand.shape, operand.dtype) for operand in operands],
            pltpu.VMEM((3, width // LANES, EDGE + rows, LANES), f32),
            pltpu.VMEM((width // LANES, rows, LANES), f32),
            pltpu.VMEM((3, EDGE, width), bf16),
            pltpu.VMEM((depth, LANES), f32),
            pltpu.VMEM((len(LEFT_PARTS) * order, LANES), f32),
            pltpu.VMEM((3 * order, LANES), f32),
            pltpu.VMEM((order, depth), bf16),
            pltpu.VMEM((order, len(LEFT_PARTS) * order), bf16),
            pltpu.VMEM((LANES, 3 * order), f32),
            pltpu.VMEM((LANES, LANES), f32),
            pltpu.VMEM((ctx, own, LANES), f32),
            pltpu.VMEM((CHUNKS, ctx, own, LANES), f32),
            pltpu.VMEM((ctx, own, 2 * LANES), f32),
            pltpu.VMEM((CHUNKS, ctx, own, 2 * LANES), f32),
            *wires,
            dma((len(operands),)),
            dma,
            dma,
            dma((CHUNKS,)),
            dma((CHUNKS, ctx)),
            dma((CHUNKS,)),
            dma((CHUNKS, ctx)),
            pltpu.SemaphoreType.REGULAR((3, 2)),
        ],
        compiler_params=pltpu.CompilerParams(
            collective_id=0, has_side_effects=True, vmem_limit_bytes=40 * 1024 * 1024
        ),
        name="hyena",
    )(*[pltpu.with_memory_space_constraint(operand, pltpu.HBM) for operand in operands])


def solution(mesh):
    placed = (
        P(None, ("dp", "ctx"), "chan"),
        P(None, None, "chan"),
        P(),
        P(),
        P(),
        P(),
        P(None, "chan"),
        P("chan"),
        P("chan"),
    )
    return jax.shard_map(
        body, mesh=mesh, in_specs=placed, out_specs=P(("dp", "ctx"), "chan"), check_vma=False
    )
```

```python
import math

import jax
import jax.numpy as jnp
import numpy as np
from jax import lax
from jax.experimental import pallas as pl
from jax.experimental.pallas import tpu as pltpu
from jax.sharding import PartitionSpec as P

BANDS = 16
TAPS = 7
LANES = 128
EDGE = 8
CHUNKS = 2
MESH = pl.DeviceIdType.MESH

OUT_POWER = 12
BACK_POWER = 10
OUT_SPAN = 248.0 / OUT_POWER
BACK_SPAN = 248.0 / BACK_POWER
OUT_LOW = 2.0 ** (-OUT_SPAN / 2)
BACK_LOW = 2.0 ** (-BACK_SPAN / 2)
OUT_REACH = (2.0**OUT_SPAN - 1.0) * OUT_LOW
BACK_REACH = (2.0**BACK_SPAN - 1.0) * BACK_LOW
LARGEST = 6.0


def position_table(total_len, rows):
    positions = np.arange(total_len, dtype=np.float32)
    bands = np.arange(1, BANDS + 1, dtype=np.float32)
    angles = positions[None, :] * bands[:, None] * np.float32(2.0 * math.pi / total_len)
    angles = angles.astype(np.float32).astype(np.float64)
    table = np.zeros((rows, total_len), np.float32)
    table[0] = positions / np.float32(total_len)
    table[1 : 1 + BANDS] = np.cos(angles)
    table[1 + BANDS : 1 + 2 * BANDS] = np.sin(angles)
    table[1 + 2 * BANDS] = 1.0
    return table


def two_parts(table):
    high = table.astype(jnp.bfloat16)
    low = (table - high.astype(np.float64)).astype(jnp.bfloat16)
    return high, low


LEFT_PARTS = (0, 0, 1, 0, 1, 2)
RIGHT_PARTS = (0, 1, 0, 2, 1, 0)


def stacked_positions(total_len, rows, depth):
    table = position_table(total_len, rows).astype(np.float64)
    parts = []
    for _ in range(3):
        part = table.astype(jnp.bfloat16)
        parts.append(part)
        table = table - part.astype(np.float64)
    stack = np.concatenate([parts[at] for at in RIGHT_PARTS])
    empty = np.zeros((depth - stack.shape[0], total_len), jnp.bfloat16)
    return np.concatenate([stack, empty])


def inner_tables():
    ids = np.arange(LANES, dtype=np.float64)
    angles = 2.0 * math.pi / LANES * np.mod(ids[:, None] * ids[None, :], LANES)
    cos, sin = np.cos(angles), np.sin(angles)
    forth = np.block([[cos, -sin], [sin, cos]])
    back = np.block([[cos, sin], [-sin, cos]])
    return np.stack(two_parts(forth) + two_parts(back))


def twist_table(outer, total_len):
    angles = (
        2.0
        * math.pi
        / total_len
        * (np.arange(outer)[:, None] + 0.25)
        * np.arange(LANES)[None, :]
    )
    return np.stack([np.cos(angles), np.sin(angles)], axis=1).astype(np.float32)


def turned(real, imag, cos, sin):
    if abs(sin) < 1e-12 and cos > 0:
        return real, imag
    if abs(cos) < 1e-12:
        return (-imag, real) if sin > 0 else (imag, -real)
    if abs(abs(cos) - abs(sin)) < 1e-12 and cos > 0:
        half = math.sqrt(0.5)
        if sin > 0:
            return (real - imag) * half, (real + imag) * half
        return (real + imag) * half, (imag - real) * half
    return real * cos - imag * sin, real * sin + imag * cos


def short_fourier(items, sign):
    size = len(items)
    if size == 1:
        return items
    even = short_fourier(items[0::2], sign)
    odd = short_fourier(items[1::2], sign)
    first, second = [], []
    for at in range(size // 2):
        angle = sign * 2.0 * math.pi * at / size
        real, imag = turned(odd[at][0], odd[at][1], math.cos(angle), math.sin(angle))
        first.append((even[at][0] + real, even[at][1] + imag))
        second.append((even[at][0] - real, even[at][1] - imag))
    return first + second


def sine(x):
    turns = jnp.round(x * (1.0 / math.pi))
    r = x - turns * 3.140625
    r = r - turns * 9.67502593994140625e-4
    r = r - turns * 1.509957990978376432e-7
    s = r * r
    poly = -2.38898859e-8 * s + 2.75255613e-6
    poly = poly * s - 1.98408743e-4
    poly = poly * s + 8.33333310e-3
    poly = poly * s - 1.66666667e-1
    value = r + r * s * poly
    half = turns * 0.5
    odd = half - jnp.floor(half)
    return value * (1.0 - 4.0 * odd)


def coded(value, scale, low, power):
    w = low + jnp.abs(value) * scale
    two = w * w
    four = two * two
    eight = four * four
    if power == 12:
        top = eight * four
    else:
        top = eight * two
    return jnp.where(value < 0, -top, top)


def decoded(code, low, power):
    w = jnp.exp(jnp.log(jnp.abs(code)) * (1.0 / power)) - low
    return jnp.where(code < 0, -w, w)


def kernel(
    ctx,
    feat_rows,
    proj_any,
    weight_any,
    *refs,
):
    (
        pos_in_any,
        pos_bias_any,
        sine_freq_any,
        pos_mid_any,
        pos_out_any,
        decay_any,
        skip_any,
        feats_any,
        inner_any,
        twist_any,
        out,
        proj,
        weight,
        pos_in,
        pos_bias,
        sine_freq,
        pos_mid,
        pos_out,
        decay,
        skip,
        feats,
        inner,
        twist,
        wide,
        driven,
        rim,
        first_w,
        second_w,
        third_w,
        first_t,
        second_t,
        third_t,
        own_decay,
        values,
        taps,
        spec,
        filt,
        send_f,
        got_f,
        send_r,
        got_r,
        local_sem,
        rim_send,
        rim_recv,
        f_send,
        f_recv,
        r_send,
        r_recv,
        news,
    ) = refs
    me = lax.axis_index("ctx")
    chip = lax.div(me, 2)
    core = lax.rem(me, 2)
    chips = ctx // 2
    rows = proj.shape[1]
    own = got_f.shape[2]
    total_len = ctx * rows

    early = ((weight_any, weight), (proj_any, proj))
    late = (
        (pos_in_any, pos_in),
        (pos_bias_any, pos_bias),
        (sine_freq_any, sine_freq),
        (pos_mid_any, pos_mid),
        (pos_out_any, pos_out),
        (decay_any, decay),
        (skip_any, skip),
        (feats_any, feats),
        (inner_any, inner),
        (twist_any, twist),
    )
    fetches = [
        pltpu.make_async_copy(there, here, local_sem.at[i])
        for i, (there, here) in enumerate(early + late)
    ]
    for fetch in fetches[: len(early)]:
        fetch.start()

    barrier = pltpu.get_barrier_semaphore()

    right = lax.rem(chip + 1, chips)
    left = lax.rem(chip + chips - 1, chips)

    def tell(sem, to):
        pl.semaphore_signal(sem, inc=1, device_id={"ctx": to}, device_id_type=MESH)

    near = (2 * chip + 1 - core, 2 * left, 2 * left + 1, 2 * right, 2 * right + 1)
    for to in near:
        tell(barrier, to)

    def slab(n):
        return pl.ds(pl.multiple_of(n * LANES, LANES), LANES)

    def taps_sum(stream, n, start, count):
        total = None
        for tap in range(TAPS):
            part = weight[stream, pl.ds(tap, 1), slab(n)] * wide[
                stream, n, EDGE + start - tap : EDGE + start - tap + count, :
            ]
            total = part if total is None else total + part
        return total

    pl.semaphore_wait(barrier, len(near))

    def rim_copy(stream):
        return pltpu.make_async_remote_copy(
            src_ref=proj_any.at[stream, pl.ds(rows - EDGE, EDGE), :],
            dst_ref=rim.at[stream],
            send_sem=rim_send.at[stream],
            recv_sem=rim_recv.at[stream],
            device_id={"ctx": lax.rem(me + 1, ctx)},
            device_id_type=MESH,
        )

    def rim_start(*streams):
        @pl.when(me < ctx - 1)
        def _():
            for stream in streams:
                rim_copy(stream).start()

    def rim_wait(*streams):
        @pl.when(me > 0)
        def _():
            for stream in streams:
                rim_copy(stream).wait_recv()

    def spread(step):
        away = 2**step
        tell(news.at[step, 0], 2 * lax.rem(chip + away, chips) + core)
        tell(news.at[step, 1], 2 * lax.rem(chip + chips - away, chips) + core)

    def hear(step):
        for side in range(2):
            pl.semaphore_wait(news.at[step, side], 1)

    spread(0)

    rim_start(0, 2)

    for fetch in fetches[: len(early)]:
        fetch.wait()
    for fetch in fetches[len(early) :]:
        fetch.start()

    def widen(n, carry):
        for stream in range(3):
            wide[stream, n, EDGE : EDGE + rows, :] = proj[stream, :, slab(n)].astype(jnp.float32)
        driven[n, EDGE:rows, :] = taps_sum(0, n, EDGE, rows - EDGE) * taps_sum(
            2, n, EDGE, rows - EDGE
        )
        return carry

    lax.fori_loop(0, chips // 2, widen, 0)
    hear(0)
    spread(1)
    lax.fori_loop(chips // 2, chips, widen, 0)
    hear(1)
    spread(2)

    @pl.when(me == 0)
    def _():
        rim[...] = jnp.zeros_like(rim)

    rim_wait(0, 2)

    def forth(g, to):
        return pltpu.make_async_remote_copy(
            src_ref=send_f.at[g, to],
            dst_ref=got_f.at[g, me],
            send_sem=f_send.at[g],
            recv_sem=f_recv.at[g, me],
            device_id={"ctx": to},
            device_id_type=MESH,
        )

    def back(g, to):
        return pltpu.make_async_remote_copy(
            src_ref=send_r.at[g, to],
            dst_ref=got_r.at[g, me],
            send_sem=r_send.at[g],
            recv_sem=r_recv.at[g, me],
            device_id={"ctx": to},
            device_id_type=MESH,
        )

    def to_chip(i):
        far = chips // 2 - lax.div(i + 1, 2)
        away = jnp.where(lax.rem(i, 2) == 1, far, chips - far)
        return lax.rem(chip + away, chips)

    def bound(n):
        total = 1.0
        for stream in (0, 2):
            size = None
            for tap in range(TAPS):
                part = jnp.abs(weight[stream, pl.ds(tap, 1), slab(n)])
                size = part if size is None else size + part
            total = total * (size * LARGEST)
        return jnp.maximum(total, 1e-30)

    def push(make, g, n):
        for c in range(2):
            to = 2 * n + c

            @pl.when(to != me)
            def _():
                make(g, to).start()

    def encode(n):
        for stream in (0, 2):
            wide[stream, n, 0:EDGE, :] = rim[stream, :, slab(n)].astype(jnp.float32)
        driven[n, 0:EDGE, :] = taps_sum(0, n, 0, EDGE) * taps_sum(2, n, 0, EDGE)
        code = coded(driven[n], OUT_REACH / bound(n), OUT_LOW, OUT_POWER)
        code = code.T.astype(jnp.bfloat16)
        for c in range(2):
            for g in range(CHUNKS):
                low = (c * CHUNKS + g) * own
                send_f[g, 2 * n + c] = code[low : low + own]
        push(forth, 0, n)

    def around(first):
        def step(i, carry):
            away = first - lax.div(i, 2)
            away = jnp.where(lax.rem(i, 2) == 0, away, chips - away)
            encode(lax.rem(chip + away, chips))
            return carry

        return step

    quarter = chips // 4
    lax.fori_loop(0, 2 * quarter, around(quarter), 0)
    encode(chip)
    hear(2)
    encode(lax.rem(chip + 2 * quarter, chips))
    lax.fori_loop(0, 2 * quarter - 2, around(2 * quarter - 1), 0)

    def rest(g, make):
        def step(i, carry):
            push(make, g, to_chip(i))
            return carry

        lax.fori_loop(0, chips, step, 0)

    for g in range(1, CHUNKS):
        rest(g, forth)
    rim_start(1)
    for g in range(CHUNKS):
        got_f[g, me] = send_f[g, me]

    for fetch in fetches[len(early) :]:
        fetch.wait()
    taps_in = pos_in.shape[0]
    order = pos_mid.shape[0]
    freq = sine_freq[...]

    def halves(x):
        high = x.astype(jnp.bfloat16)
        return high, (x - high.astype(jnp.float32)).astype(jnp.bfloat16)

    def thirds(x):
        high, low = halves(x)
        rest_of = x - high.astype(jnp.float32)
        return high, low, (rest_of - low.astype(jnp.float32)).astype(jnp.bfloat16)

    first_w[...] = jnp.zeros_like(first_w)
    second_w[...] = jnp.zeros_like(second_w)
    third_w[...] = jnp.zeros_like(third_w)
    entry = thirds(pos_in[...] * freq)
    offset = thirds(pos_bias[...] * freq)
    middle = thirds(pos_mid[...] * freq)
    exit_high, exit_low = halves(pos_out[:, slab(chip)])
    for i, part in enumerate(LEFT_PARTS):
        at = i * feat_rows
        first_w[at : at + taps_in, 0:order] = entry[part].astype(jnp.float32)
        first_w[at + taps_in : at + taps_in + 1, 0:order] = offset[part].astype(jnp.float32)
        second_w[i * order : (i + 1) * order, 0:order] = middle[part].astype(jnp.float32)
    for i, part in enumerate((exit_high, exit_low, exit_high)):
        third_w[i * order : (i + 1) * order, :] = part.astype(jnp.float32)
    first_t[...] = first_w[...].T[0:order].astype(jnp.bfloat16)
    second_t[...] = second_w[...].T[0:order].astype(jnp.bfloat16)
    third_t[...] = third_w[...].T
    own_decay[...] = jnp.broadcast_to(decay[:, slab(chip)], (LANES, LANES)).T

    mine = pl.ds(pl.multiple_of(core * (CHUNKS * own), CHUNKS * own), CHUNKS * own)
    third = third_t[mine, :].astype(jnp.bfloat16)
    rate = own_decay[mine, :]
    span = 512

    def network(j, squares):
        at = pl.ds(pl.multiple_of(j * span, span), span)
        one = thirds(sine(jnp.dot(first_t[...], feats[:, at], preferred_element_type=jnp.float32)))
        one = jnp.concatenate([one[part] for part in RIGHT_PARTS], axis=0)
        two = sine(jnp.dot(second_t[...], one, preferred_element_type=jnp.float32))
        high, low = halves(two)
        two = jnp.concatenate([high, high, low], axis=0)
        raw = jnp.dot(third, two, preferred_element_type=jnp.float32)
        for i in range(span // LANES):
            a = j * (span // LANES) + i
            place = lax.broadcasted_iota(jnp.int32, (CHUNKS * own, LANES), 1) + a * LANES
            long_filter = raw[:, i * LANES : (i + 1) * LANES] * jnp.exp(
                -(rate * place.astype(jnp.float32))
            )
            for g in range(CHUNKS):
                taps[g, a] = long_filter[g * own : (g + 1) * own]
            squares = squares + long_filter * long_filter
        return squares

    squares = lax.fori_loop(
        0, total_len // span, network, jnp.zeros((CHUNKS * own, LANES), jnp.float32)
    )
    norm = jnp.sqrt(jnp.sum(squares, axis=1, keepdims=True) + 1e-05)
    scale = (1.0 / total_len) / norm

    group = 8

    def product(x, which):
        high, low = halves(x)
        return (
            jnp.dot(high, inner[which], preferred_element_type=jnp.float32)
            + jnp.dot(low, inner[which], preferred_element_type=jnp.float32)
            + jnp.dot(high, inner[which + 1], preferred_element_type=jnp.float32)
        )

    def outer_forth(source):
        def step(j, carry):
            at = pl.ds(pl.multiple_of(j * group, group), group)
            items = []
            for a in range(ctx):
                x = source[a, at, :]
                angle = 2.0 * math.pi * a / (4 * ctx)
                items.append((x * math.cos(angle), x * -math.sin(angle)))
            for k, (real, imag) in enumerate(short_fourier(items, -1)):
                cos, sin = twist[k, 0:1, :], twist[k, 1:2, :]
                spec[k, at, 0:LANES] = real * cos + imag * sin
                spec[k, at, LANES : 2 * LANES] = imag * cos - real * sin
            return carry

        lax.fori_loop(0, own // group, step, 0)

    def outer_back():
        def step(j, carry):
            at = pl.ds(pl.multiple_of(j * group, group), group)
            items = []
            for k in range(ctx):
                real, imag = spec[k, at, 0:LANES], spec[k, at, LANES : 2 * LANES]
                cos, sin = twist[k, 0:1, :], twist[k, 1:2, :]
                items.append((real * cos - imag * sin, imag * cos + real * sin))
            for a, (real, imag) in enumerate(short_fourier(items, 1)):
                angle = 2.0 * math.pi * a / (4 * ctx)
                values[a, at, :] = real * math.cos(angle) - imag * math.sin(angle)
            return carry

        lax.fori_loop(0, own // group, step, 0)

    for g in range(CHUNKS):
        outer_forth(taps.at[g])
        full = product(spec[...].reshape(ctx * own, 2 * LANES), 0)
        filt[g] = full.reshape(ctx, own, 2 * LANES) * scale[None, g * own : (g + 1) * own]

    for g in range(CHUNKS):

        def arrive(i, carry):
            frm = lax.rem(me + i, ctx)
            pltpu.make_async_remote_copy(
                src_ref=send_f.at[g, frm],
                dst_ref=got_f.at[g, frm],
                send_sem=f_send.at[g],
                recv_sem=f_recv.at[g, frm],
                device_id={"ctx": frm},
                device_id_type=MESH,
            ).wait_recv()
            return carry

        lax.fori_loop(1, ctx, arrive, 0)

        def decode(a, carry):
            values[a] = decoded(got_f[g, a].astype(jnp.float32), OUT_LOW, OUT_POWER)
            return carry

        lax.fori_loop(0, ctx, decode, 0)
        outer_forth(values)
        full = product(spec[...].reshape(ctx * own, 2 * LANES), 0)
        real, imag = full[:, :LANES], full[:, LANES:]
        response = filt[g].reshape(ctx * own, 2 * LANES)
        f_real, f_imag = response[:, :LANES], response[:, LANES:]
        mixed_real = real * f_real - imag * f_imag
        mixed_imag = real * f_imag + imag * f_real
        full = product(jnp.concatenate([mixed_real, mixed_imag], axis=1), 2)
        spec[...] = full.reshape(ctx, own, 2 * LANES)
        outer_back()

        def pack(i, carry):
            n = to_chip(i)
            for c in range(2):
                a = 2 * n + c
                code = coded(values[a], BACK_REACH / (64.0 * OUT_REACH), BACK_LOW, BACK_POWER)
                send_r[g, a] = code.astype(jnp.bfloat16)
            push(back, g, n)
            return carry

        lax.fori_loop(0, chips, pack, 0)
        got_r[g, me] = send_r[g, me]

    rim_wait(1)

    def gate(n, carry):
        wide[1, n, 0:EDGE, :] = rim[1, :, slab(n)].astype(jnp.float32)
        wide[1, n, EDGE : EDGE + rows, :] = taps_sum(1, n, 0, rows)
        return carry

    lax.fori_loop(0, chips, gate, 0)

    def finish(i, carry):
        n = to_chip(i)
        parts = []
        for c in range(2):
            frm = 2 * n + c
            for g in range(CHUNKS):

                @pl.when(frm != me)
                def _():
                    pltpu.make_async_remote_copy(
                        src_ref=send_r.at[g, frm],
                        dst_ref=got_r.at[g, frm],
                        send_sem=r_send.at[g],
                        recv_sem=r_recv.at[g, frm],
                        device_id={"ctx": frm},
                        device_id_type=MESH,
                    ).wait_recv()

        for c in range(2):
            for g in range(CHUNKS):
                parts.append(got_r[g, 2 * n + c].astype(jnp.float32))
        code = jnp.concatenate(parts, axis=0).T
        unit = bound(n) * (64.0 / BACK_REACH)
        long_conv = decoded(code, BACK_LOW, BACK_POWER) * unit
        right = wide[1, n, EDGE : EDGE + rows, :]
        mixed = right * (long_conv + skip[:, slab(n)] * driven[n])
        out[:, slab(n)] = mixed.astype(jnp.bfloat16)
        return carry

    lax.fori_loop(0, chips, finish, 0)

    @pl.when(me < ctx - 1)
    def _():
        for stream in range(3):
            rim_copy(stream).wait_send()

    for g in range(CHUNKS):
        for buffer, sem in ((send_f, f_send), (send_r, r_send)):
            sent = buffer.at[g, pl.ds(0, ctx - 1)]
            pltpu.make_async_remote_copy(
                src_ref=sent,
                dst_ref=sent,
                send_sem=sem.at[g],
                recv_sem=sem.at[g],
                device_id={"ctx": me},
                device_id_type=MESH,
            ).wait_send()


def body(
    projected, short_weight, pos_in, pos_bias, sine_freq, pos_mid, pos_out, decay_rate, skip_gain
):
    ctx = lax.axis_size("ctx")
    _, rows, width = projected.shape
    own = width // ctx // CHUNKS
    order = pos_mid.shape[0]
    total_len = ctx * rows
    feat_rows = -(-(pos_in.shape[0] + 1) // 8) * 8
    depth = -(-feat_rows * len(LEFT_PARTS) // 256) * 256
    feats = jnp.asarray(stacked_positions(total_len, feat_rows, depth))
    inner = jnp.asarray(inner_tables())
    twist = jnp.asarray(twist_table(ctx, total_len))
    vmem = pl.BlockSpec(memory_space=pltpu.VMEM)
    left = pl.BlockSpec(memory_space=pltpu.HBM)
    bf16, f32 = jnp.bfloat16, jnp.float32
    dma = pltpu.SemaphoreType.DMA
    wires = [pltpu.VMEM((CHUNKS, ctx, own, rows), bf16)] * 4

    def call(*refs):
        return kernel(ctx, feat_rows, *refs)

    operands = (
        projected,
        short_weight.transpose(1, 0, 2),
        pos_in,
        pos_bias.reshape(1, -1),
        sine_freq.reshape(1, -1),
        pos_mid,
        pos_out,
        decay_rate.reshape(1, -1),
        skip_gain.reshape(1, -1),
        feats,
        inner,
        twist,
    )
    return pl.pallas_call(
        call,
        out_shape=jax.ShapeDtypeStruct((rows, width), bf16),
        in_specs=[left] * 12,
        out_specs=vmem,
        scratch_shapes=[
            *[pltpu.VMEM(operand.shape, operand.dtype) for operand in operands],
            pltpu.VMEM((3, width // LANES, EDGE + rows, LANES), f32),
            pltpu.VMEM((width // LANES, rows, LANES), f32),
            pltpu.VMEM((3, EDGE, width), bf16),
            pltpu.VMEM((depth, LANES), f32),
            pltpu.VMEM((len(LEFT_PARTS) * order, LANES), f32),
            pltpu.VMEM((3 * order, LANES), f32),
            pltpu.VMEM((order, depth), bf16),
            pltpu.VMEM((order, len(LEFT_PARTS) * order), bf16),
            pltpu.VMEM((LANES, 3 * order), f32),
            pltpu.VMEM((LANES, LANES), f32),
            pltpu.VMEM((ctx, own, LANES), f32),
            pltpu.VMEM((CHUNKS, ctx, own, LANES), f32),
            pltpu.VMEM((ctx, own, 2 * LANES), f32),
            pltpu.VMEM((CHUNKS, ctx, own, 2 * LANES), f32),
            *wires,
            dma((len(operands),)),
            dma((3,)),
            dma((3,)),
            dma((CHUNKS,)),
            dma((CHUNKS, ctx)),
            dma((CHUNKS,)),
            dma((CHUNKS, ctx)),
            pltpu.SemaphoreType.REGULAR((3, 2)),
        ],
        compiler_params=pltpu.CompilerParams(
            collective_id=0, has_side_effects=True, vmem_limit_bytes=40 * 1024 * 1024
        ),
        name="hyena",
    )(*[pltpu.with_memory_space_constraint(operand, pltpu.HBM) for operand in operands])


def solution(mesh):
    placed = (
        P(None, ("dp", "ctx"), "chan"),
        P(None, None, "chan"),
        P(),
        P(),
        P(),
        P(),
        P(None, "chan"),
        P("chan"),
        P("chan"),
    )
    return jax.shard_map(
        body, mesh=mesh, in_specs=placed, out_specs=P(("dp", "ctx"), "chan"), check_vma=False
    )
```
